32 devices in a mesh: state: 8 (over z, y), mem: 4 (over x, core).
Axes of the slice: x: 2, y: 2, z: 4, core: 2. Of those that a mesh axis runs over, the one named last changes fastest.
Arguments:
- background_matrix: float32 [80, 524288], P('mem', 'state'), may hold values from -6 to 6
- measured_readings: float32 [4, 192], replicated, may hold values from -8 to 8
- measurement_noise: float32 [4, 192], replicated, may hold values from 0.5 to 2
- holding_processor: int32 [4], replicated, may hold values from 0 to 31
- measured_position: int32 [4, 192], replicated, may hold values from 0 to 16383
- taper_grade: int32 [4, 192, 1024], P(None, None, ('state', 'mem')), may hold values from 0 to 4
Outputs:
- analysis: float32 [80, 524288], P(None, ('state', 'mem'))
The draws below stay inside these ranges and needn't reach their ends.
Inputs may be any that keep to these rules, and one draw needn't show every extreme that they name: `holding_processor`: batches may share an owner; observations of a batch may share a variable.
All inputs are finite; a program needn't handle non-finite values.
Results may differ from the reference program's by a relative error of at most 0.0003.
Values sent between devices are 32-bit elements; how exact they have to be, the bound alone decides.
No kernel may reach another device: no remote copies, remote signals or barrier semaphores. Data moves between devices by JAX's collectives and lax.ppermute only.
A program may use at most 256 MiB of HBM per device.

```python
import math
import jax
import jax.numpy as jnp
from jax import lax

REALIZATIONS = 80
UNIT_VARIABLES = 16384
BLK = 512
OBS = 192
BATCHES = 4
GLOBAL_UNKNOWNS = 524288
NBLK = 1024
N_STATE = 8
N_MEM = 4


def place_ends(entries, rng, least, top_value):
    place = [jax.random.randint(jax.random.fold_in(rng, axis), (), 0, length) for axis, length in enumerate(entries.shape)]
    main_axis = entries.shape.index(max(entries.shape))
    next_to = place[:main_axis] + [(place[main_axis] + 1) % entries.shape[main_axis]] + place[main_axis + 1:]
    return entries.at[tuple(place)].set(least).at[tuple(next_to)].set(top_value)


def block_levels(rng, shape, cuts, low, largest):
    def one(axis_at, shards_of):
        steps = jax.random.uniform(jax.random.fold_in(jax.random.fold_in(rng, 6), axis_at), (shards_of,), jnp.float32, low / len(cuts), largest / len(cuts))
        return jnp.repeat(jnp.exp(steps), shape[axis_at] // shards_of).reshape((-1,) + (1,) * (len(shape) - axis_at - 1))

    level = one(*cuts[0])
    for cut in cuts[1:]:
        level = level * one(*cut)
    return level


def normal_values(stream_key, dims, scale, limit, split=(), kind=jnp.bfloat16):
    entries = scale * jax.random.normal(stream_key, dims, jnp.float32)
    if split:
        entries = entries * block_levels(stream_key, dims, split, -0.22, 0.18)
    return jnp.clip(entries, -limit, limit).astype(kind)


def setup_inputs(seed: int = 0) -> dict:
    arg_keys = jax.random.split(jax.random.key(seed), 7)
    return {
        "background_matrix": normal_values(arg_keys[0], (REALIZATIONS, GLOBAL_UNKNOWNS), 1.0, 6.0, ((0, 4), (1, 8)), jnp.float32),
        "measured_readings": normal_values(arg_keys[1], (BATCHES, OBS), 1.5, 8.0, (), jnp.float32),
        "measurement_noise": jnp.clip(jnp.exp(jax.random.uniform(arg_keys[2], (BATCHES, OBS), jnp.float32, math.log(0.5), math.log(2.0))), 0.5, 2.0),
        "holding_processor": place_ends(jax.random.randint(arg_keys[3], (BATCHES,), 0, N_STATE * N_MEM), jax.random.fold_in(arg_keys[3], 1), 0, (N_STATE * N_MEM) - 1).astype(jnp.int32),
        "measured_position": place_ends(jax.random.randint(arg_keys[4], (BATCHES, OBS), 0, UNIT_VARIABLES), jax.random.fold_in(arg_keys[4], 1), 0, UNIT_VARIABLES - 1).astype(jnp.int32),
        "taper_grade": place_ends(jax.random.randint(arg_keys[5], (BATCHES, OBS, NBLK), 0, 5), jax.random.fold_in(arg_keys[5], 1), 0, 4).astype(jnp.int32),
    }


PRECISE = lax.Precision.HIGHEST

def system_inverse(prior, errors):
    spread = prior - jnp.mean(prior, axis=0)
    system = jnp.dot(spread.T, spread, precision=PRECISE) / (prior.shape[0] - 1) + jnp.diag(errors)
    factor = jnp.linalg.cholesky(system)
    identity = jnp.eye(system.shape[0], dtype=system.dtype)
    lower_inv = lax.linalg.triangular_solve(factor, identity, left_side=True, lower=True)
    return jnp.dot(lower_inv.T, lower_inv, precision=PRECISE)

def expand_levels(levels):
    scaled = levels.astype(jnp.float32) / 4.0
    widened = scaled[:, :, None] * jnp.ones((BLK,), jnp.float32)
    return widened.reshape(levels.shape[0], levels.shape[1] * BLK)

def update_columns(realization_slab, taper, spread, innovation, inverse):
    center = jnp.mean(realization_slab, axis=0, keepdims=True)
    anomaly = realization_slab - center
    cov = jnp.dot(spread.T, anomaly, precision=PRECISE) / (realization_slab.shape[0] - 1)
    weights = jnp.dot(inverse, taper * cov, precision=PRECISE)
    center = center + jnp.dot(innovation[None, :], weights, precision=PRECISE)
    anomaly = anomaly - 0.5 * jnp.dot(spread, weights, precision=PRECISE)
    return center + anomaly

def reference(background_matrix, measured_readings, measurement_noise, holding_processor, measured_position, taper_grade):
    processor_roster = N_STATE * N_MEM
    realization_lines = background_matrix.shape[0]
    realization_sets = background_matrix.reshape(realization_lines, processor_roster, UNIT_VARIABLES).transpose(1, 0, 2)
    levels = taper_grade.reshape(BATCHES, OBS, processor_roster, UNIT_VARIABLES // BLK).transpose(2, 0, 1, 3)
    for batch in range(BATCHES):
        block = lax.dynamic_index_in_dim(realization_sets, holding_processor[batch].astype(jnp.int32), 0, keepdims=False)
        prior = jnp.take(block, measured_position[batch], axis=1)
        center = jnp.mean(prior, axis=0)
        spread = prior - center
        innovation = measured_readings[batch] - center
        inverse = system_inverse(prior, measurement_noise[batch])

        def one_group(pair, batch=batch, spread=spread, innovation=innovation, inverse=inverse):
            realization_slab, level_group = pair
            return update_columns(realization_slab, expand_levels(level_group[batch]), spread, innovation, inverse)
        realization_sets = lax.map(one_group, (realization_sets, levels))
    return realization_sets.transpose(1, 0, 2).reshape(realization_lines, processor_roster * UNIT_VARIABLES)
```

```python
import functools

import jax
import jax.numpy as jnp
from jax import lax
from jax.experimental import pallas as pl
from jax.experimental.pallas import tpu as pltpu
from jax.sharding import PartitionSpec as P

LANES = 128
SUBLANES = 8
EXACT = lax.Precision.HIGHEST
NN = (((1,), (0,)), ((), ()))
NT = (((1,), (1,)), ((), ()))
TN = (((0,), (0,)), ((), ()))
VMEM_LIMIT = 56 * 1024 * 1024


def dot32(a, b, dims=NN):
    return lax.dot_general(a, b, dims, precision=EXACT, preferred_element_type=jnp.float32)


def dot16(a, b, dims=NN):
    return lax.dot_general(a, b, dims, preferred_element_type=jnp.float32)


def split(x):
    high = x.astype(jnp.bfloat16)
    return high, (x - high.astype(jnp.float32)).astype(jnp.bfloat16)


def dot3(a, b, dims=NN):
    return dot16(a[0], b[0], dims) + (dot16(a[0], b[1], dims) + dot16(a[1], b[0], dims))


class Sizes:
    def __init__(self, mesh, background, position, grade):
        self.n_state, self.n_mem = mesh.shape["state"], mesh.shape["mem"]
        self.rows = background.shape[0]
        self.unit = background.shape[1] // self.n_mem
        self.members = self.rows * self.n_mem
        self.batches, self.obs = position.shape
        self.blocks = grade.shape[2]
        self.width = self.unit // self.blocks
        self.whole = self.rows // SUBLANES * SUBLANES
        self.rest = self.rows - self.whole
        self.fold = self.whole // self.rest
        self.packed = self.unit + self.unit // self.fold
        self.tiles = self.batches * self.obs // LANES
        self.pairs = [(b, c) for c in range(self.batches) for b in range(c)]
        self.grade_rows = len(self.pairs) * self.blocks
        self.tail = self.obs - LANES
        assert self.batches * self.obs % LANES == 0 and 2 * self.tail == LANES
        assert self.rest and self.whole % self.rest == 0 and self.unit % (self.fold * self.width) == 0


def gather_kernel(z, owner_ref, pos_ref, bg_ref, grade_ref, p_ref, g_ref, slab, gbuf, sems, gsem):
    me_state, me_mem = lax.axis_index("state"), lax.axis_index("mem")
    me = me_state * z.n_mem + me_mem
    levels = pltpu.make_async_copy(grade_ref, gbuf, gsem)
    levels.start()

    def slab_copy(b):
        at = pl.multiple_of(lax.rem(owner_ref[b], z.n_mem) * z.unit, LANES)
        return pltpu.make_async_copy(bg_ref.at[:, pl.ds(at, z.unit)], slab.at[b], sems.at[b])

    here = [lax.div(owner_ref[b], z.n_mem) == me_state for b in range(z.batches)]
    for b in range(z.batches):
        pl.when(here[b])(lambda b=b: slab_copy(b).start())
    p_ref[...] = jnp.zeros_like(p_ref)
    levels.wait()
    for n, (b, c) in enumerate(z.pairs):
        mine = jnp.where(owner_ref[c] == me, 1.0, 0.0)
        g = gbuf[b].astype(jnp.float32) * mine
        g_ref[n * z.blocks:(n + 1) * z.blocks, :] = g[:, :LANES]
        half, r0 = n // (len(z.pairs) // 2), (n % (len(z.pairs) // 2)) * z.blocks + z.grade_rows
        g_ref[r0:r0 + z.blocks, half * z.tail:(half + 1) * z.tail] = g[:, LANES:]
    lane = lax.broadcasted_iota(jnp.int32, (z.rows, LANES), 1)

    def take(b):
        slab_copy(b).wait()
        first = b * z.obs
        while first < (b + 1) * z.obs:
            last = min((first // LANES + 1) * LANES, (b + 1) * z.obs)

            def body(q, acc):
                p = pos_ref[b, q - b * z.obs]
                at = pl.multiple_of(lax.div(p, LANES) * LANES, LANES)
                tile = slab[b, :, pl.ds(at, LANES)]
                to = lax.rem(q, LANES)
                tile = pltpu.roll(tile, lax.rem(to - p + at + LANES, LANES), 1)
                return jnp.where(lane == to, tile, acc)

            t = first // LANES
            acc = p_ref[t * z.rows:(t + 1) * z.rows, :]
            p_ref[t * z.rows:(t + 1) * z.rows, :] = lax.fori_loop(first, last, body, acc, unroll=16)
            first = last

    for b in range(z.batches):
        pl.when(here[b])(functools.partial(take, b))


def gather(z, owner, position, background, grade):
    return pl.pallas_call(
        functools.partial(gather_kernel, z),
        out_shape=(
            jax.ShapeDtypeStruct((z.tiles * z.rows, LANES), jnp.float32),
            jax.ShapeDtypeStruct((z.grade_rows * z.obs // LANES, LANES), jnp.float32),
        ),
        in_specs=[
            pl.BlockSpec(memory_space=pltpu.SMEM),
            pl.BlockSpec(memory_space=pltpu.SMEM),
            pl.BlockSpec(memory_space=pl.ANY),
            pl.BlockSpec(memory_space=pl.ANY),
        ],
        out_specs=(pl.BlockSpec(memory_space=pltpu.VMEM), pl.BlockSpec(memory_space=pltpu.VMEM)),
        scratch_shapes=[
            pltpu.VMEM((z.batches, z.rows, z.unit), jnp.float32),
            pltpu.VMEM(grade.shape, jnp.int32),
            pltpu.SemaphoreType.DMA((z.batches,)),
            pltpu.SemaphoreType.DMA,
        ],
        compiler_params=pltpu.CompilerParams(vmem_limit_bytes=VMEM_LIMIT),
        name="gather",
    )(owner, position, background, grade)


def pack_kernel(z, bg_ref, *refs):
    outs, rest, sem_w, sem_r = refs[:z.n_mem], refs[-3], refs[-2], refs[-1]
    me = lax.axis_index("mem")

    def copies(r):
        cols = pl.ds(pl.multiple_of(lax.bitwise_xor(me, r) * z.unit, LANES), z.unit)
        return (
            pltpu.make_async_copy(bg_ref.at[:z.whole, cols], outs[r].at[:, :z.unit], sem_w.at[r]),
            pltpu.make_async_copy(bg_ref.at[z.whole:, cols], rest.at[r], sem_r.at[r]),
        )

    order = list(range(1, z.n_mem)) + [0]
    for r in order:
        for copy in copies(r):
            copy.start()
    part = z.unit // z.fold
    for r in order:
        whole, tail = copies(r)
        tail.wait()
        for q in range(z.fold):
            outs[r][q * z.rest:(q + 1) * z.rest, z.unit:] = rest[r, :, q * part:(q + 1) * part]
        whole.wait()


def pack(z, background):
    shape = jax.ShapeDtypeStruct((z.whole, z.packed), jnp.float32)
    return pl.pallas_call(
        functools.partial(pack_kernel, z),
        out_shape=[shape] * z.n_mem,
        in_specs=[pl.BlockSpec(memory_space=pl.ANY)],
        out_specs=[pl.BlockSpec(memory_space=pltpu.VMEM)] * z.n_mem,
        scratch_shapes=[
            pltpu.VMEM((z.n_mem, z.rest, z.unit), jnp.float32),
            pltpu.SemaphoreType.DMA((z.n_mem,)),
            pltpu.SemaphoreType.DMA((z.n_mem,)),
        ],
        compiler_params=pltpu.CompilerParams(vmem_limit_bytes=VMEM_LIMIT),
        name="pack",
    )(background)


def serial_kernel(z, p_ref, g_ref, level_ref, y_ref, noise_ref, pos_ref, th_ref, tl_ref, pbuf, tbuf):
    n, scale = z.members, 1.0 / (z.members - 1)
    me = lax.axis_index("mem")
    for t in range(z.tiles):
        for m in range(z.n_mem):
            pbuf[m * z.rows:(m + 1) * z.rows, t * LANES:(t + 1) * LANES] = p_ref[m, t * z.rows:(t + 1) * z.rows, :]
    priors = [pbuf[:, b * z.obs:(b + 1) * z.obs] for b in range(z.batches)]
    row = lax.broadcasted_iota(jnp.int32, (n, n), 0)
    col = lax.broadcasted_iota(jnp.int32, (n, n), 1)
    eye = jnp.where(row == col, 1.0, 0.0)
    edge = z.whole * z.n_mem
    late = col >= edge
    source = jnp.where(late, lax.div(col - edge, z.rest), lax.div(col, z.whole))
    within = jnp.where(late, z.whole + lax.rem(col - edge, z.rest), lax.rem(col, z.whole))
    order = jnp.where(row == lax.bitwise_xor(source, me) * z.rows + within, 1.0, 0.0)
    block = lax.div(pos_ref[...], z.width)
    sub = lax.broadcasted_iota(jnp.int32, (z.blocks, z.obs), 0)
    pick = [jnp.where(sub == block[c:c + 1, :], 1.0, 0.0).astype(jnp.bfloat16) for c in range(z.batches)]

    def observed_levels(b, c):
        k = z.pairs.index((b, c))
        half, r0 = k // (len(z.pairs) // 2), (k % (len(z.pairs) // 2)) * z.blocks + z.grade_rows
        g = jnp.concatenate(
            [g_ref[k * z.blocks:(k + 1) * z.blocks, :], g_ref[r0:r0 + z.blocks, half * z.tail:(half + 1) * z.tail]], axis=1)
        return dot16(g.astype(jnp.bfloat16), pick[c], TN)

    for b in range(z.batches):
        prior = priors[b]
        mean = jnp.sum(prior, axis=0, keepdims=True) * (1.0 / n)
        spread = prior - mean
        innovation = y_ref[b:b + 1, :] - mean
        inv_noise = 1.0 / noise_ref[b:b + 1, :]
        weighted = spread * inv_noise
        gram = dot32(weighted, spread, NT) * scale
        shift = dot32(innovation, weighted, NT) * scale
        top = 1.0 + jnp.max(jnp.sum(jnp.abs(gram), axis=0, keepdims=True), axis=1, keepdims=True)
        first = 2.0 / (1.0 + top)
        e = (top - 1.0) / (top + 1.0)
        err = eye - first * (eye + gram)
        acc = first * (0.5 * eye + shift)

        def step(err, acc, e):
            both = dot32(jnp.concatenate([err, acc], axis=0), err)
            mu = 2.0 / (2.0 - e * e)
            return mu * both[:n] + (1.0 - mu) * eye, mu * (acc + both[n:]), e * e / (2.0 - e * e)

        for _ in range(4):
            err, acc, e = step(err, acc, e)
        err, acc, e = lax.while_loop(lambda s: jnp.max(s[2]) > 1e-3, lambda s: step(*s), (err, acc, e))
        acc = acc + dot32(acc, err)
        gain = innovation * inv_noise - dot32(acc, weighted)
        quarter = spread * (0.25 * scale)
        for c in range(b + 1, z.batches):
            priors[c] = priors[c] + dot32(gain, observed_levels(b, c) * dot32(quarter, priors[c], TN))
        right = split(dot32(order, quarter, TN) if b == 0 else quarter)

        def one_block(k, carry, b=b, gain=gain, right=right):
            left = split(gain * level_ref[b, pl.ds(k, 1), :].astype(jnp.float32))
            move = dot3(left, right, NT)
            if b == 0:
                new = order + move
            else:
                old = tbuf[k]
                new = old + dot3(split(move), split(old))
            if b + 1 < z.batches:
                tbuf[k] = new
            else:
                th_ref[k], tl_ref[k] = split(new)
            return carry

        lax.fori_loop(0, z.blocks, one_block, 0, unroll=4)


def serial(z, prior, grades, levels, readings, noise, position):
    out = jax.ShapeDtypeStruct((z.blocks, z.members, z.members), jnp.bfloat16)
    vmem = pl.BlockSpec(memory_space=pltpu.VMEM)
    return pl.pallas_call(
        functools.partial(serial_kernel, z),
        out_shape=(out, out),
        in_specs=[vmem] * 6,
        out_specs=(vmem, vmem),
        scratch_shapes=[
            pltpu.VMEM((z.members, z.tiles * LANES), jnp.float32),
            pltpu.VMEM((z.blocks, z.members, z.members), jnp.float32),
        ],
        compiler_params=pltpu.CompilerParams(vmem_limit_bytes=VMEM_LIMIT),
        name="serial",
    )(prior, grades, levels, readings, noise, position)


def apply_kernel(z, th_ref, tl_ref, *refs):
    ins, out_ref, buf, sems = refs[:z.n_mem], refs[z.n_mem], refs[-2], refs[-1]
    part = z.unit // z.fold
    per = part // z.width
    for q in range(z.fold):

        def one_block(i, carry, q=q):
            at = pl.multiple_of(i * z.width, LANES)
            wide = pl.ds(q * part + at, z.width)
            rest = pl.ds(z.unit + at, z.width)
            x = jnp.concatenate(
                [r[:, wide] for r in ins] + [r[q * z.rest:(q + 1) * z.rest, rest] for r in ins], axis=0)
            k = q * per + i
            buf[:, wide] = dot3((th_ref[k], tl_ref[k]), split(x))
            return carry

        lax.fori_loop(0, per, one_block, 0, unroll=2)
        cols = pl.ds(q * part, part)
        pltpu.make_async_copy(buf.at[:, cols], out_ref.at[:, cols], sems.at[q]).start()
    for q in range(z.fold):
        cols = pl.ds(q * part, part)
        pltpu.make_async_copy(buf.at[:, cols], out_ref.at[:, cols], sems.at[q]).wait()


def apply(z, moves, parts):
    vmem = pl.BlockSpec(memory_space=pltpu.VMEM)
    return pl.pallas_call(
        functools.partial(apply_kernel, z),
        out_shape=jax.ShapeDtypeStruct((z.members, z.unit), jnp.float32),
        in_specs=[vmem] * (2 + z.n_mem),
        out_specs=pl.BlockSpec(memory_space=pl.ANY),
        scratch_shapes=[
            pltpu.VMEM((z.members, z.unit), jnp.float32),
            pltpu.SemaphoreType.DMA((z.fold,)),
        ],
        compiler_params=pltpu.CompilerParams(vmem_limit_bytes=VMEM_LIMIT),
        name="apply",
    )(*moves, *parts)


def swap(x, axis, bit, size):
    return lax.ppermute(x, axis, [(i, i ^ bit) for i in range(size)])


def share(z, prior, grades):
    me = lax.axis_index("mem")
    half = grades.shape[0] // 2
    odd = me % 2 == 1
    low, high = grades[:half], grades[half:]
    mine = jnp.where(odd, high, low) + swap(jnp.where(odd, low, high), "mem", 1, z.n_mem)
    both = jnp.concatenate([prior, mine], axis=0)
    bit = 1
    while bit < z.n_state:
        both = both + swap(both, "state", bit, z.n_state)
        bit *= 2
    prior, mine = both[:prior.shape[0]], both[prior.shape[0]:]
    there = swap(both, "mem", 2, z.n_mem)
    other, mine = there[:prior.shape[0]], mine + there[prior.shape[0]:]
    upper = me >= 2
    pair = jnp.stack([jnp.where(upper, other, prior), jnp.where(upper, prior, other)])
    rows = pair.shape[0] * pair.shape[1]
    both = jnp.concatenate([pair.reshape(rows, LANES), mine], axis=0)
    there = swap(both, "mem", 1, z.n_mem)
    pair_t = there[:rows].reshape(pair.shape)
    mine_t = there[rows:]
    even, uneven = jnp.where(odd, pair_t, pair), jnp.where(odd, pair, pair_t)
    prior = jnp.stack([even[0], uneven[0], even[1], uneven[1]])
    grades = jnp.concatenate([jnp.where(odd, mine_t, mine), jnp.where(odd, mine, mine_t)], axis=0)
    return prior, grades


def solution(mesh):
    def local(background, readings, noise, owner, position, grade):
        z = Sizes(mesh, background, position, grade)
        levels = jnp.transpose(grade, (0, 2, 1))
        parts = pack(z, background)
        parts = [parts[0]] + [swap(parts[r], "mem", r, z.n_mem) for r in range(1, z.n_mem)]
        prior, grades = gather(z, owner, position, background, levels)
        prior, grades = share(z, prior, grades)
        moves = serial(z, prior, grades, levels, readings, noise, position)
        return apply(z, moves, parts)

    return jax.shard_map(
        local,
        mesh=mesh,
        in_specs=(P("mem", "state"), P(), P(), P(), P(), P(None, None, ("state", "mem"))),
        out_specs=P(None, ("state", "mem")),
        check_vma=False,
    )
```

```python
import functools

import jax
import jax.numpy as jnp
from jax import lax
from jax.experimental import pallas as pl
from jax.experimental.pallas import tpu as pltpu
from jax.sharding import PartitionSpec as P


LANES = 128
SUBLANES = 8
EXACT = lax.Precision.HIGHEST
NN = (((1,), (0,)), ((), ()))
NT = (((1,), (1,)), ((), ()))
TN = (((0,), (0,)), ((), ()))
MIB = 1024 * 1024
GROUP = 4


def dot32(a, b, dims=NN):
    return lax.dot_general(a, b, dims, precision=EXACT, preferred_element_type=jnp.float32)


def dot16(a, b, dims=NN):
    return lax.dot_general(a, b, dims, preferred_element_type=jnp.float32)


def split(x):
    high = x.astype(jnp.bfloat16)
    return high, (x - high.astype(jnp.float32)).astype(jnp.bfloat16)


def dot3(a, b, dims=NN):
    return dot16(a[0], b[0], dims) + (dot16(a[0], b[1], dims) + dot16(a[1], b[0], dims))


class Sizes:
    def __init__(self, mesh, background, position, grade):
        self.n_state, self.n_mem = mesh.shape["state"], mesh.shape["mem"]
        self.rows = background.shape[0]
        self.unit = background.shape[1] // self.n_mem
        self.members = self.rows * self.n_mem
        self.batches, self.obs = position.shape
        self.blocks = grade.shape[2]
        self.width = self.unit // self.blocks
        self.whole = self.rows // SUBLANES * SUBLANES
        self.rest = self.rows - self.whole
        self.fold = self.whole // self.rest
        self.packed = self.unit + self.unit // self.fold
        self.tiles = self.batches * self.obs // LANES
        self.pairs = [(b, c) for c in range(self.batches) for b in range(c)]
        self.grade_rows = len(self.pairs) * self.blocks
        self.tail = self.obs - LANES
        assert self.batches * self.obs % LANES == 0 and 2 * self.tail == LANES
        assert self.rest and self.whole % self.rest == 0 and self.unit % (self.fold * self.width) == 0


def gather_kernel(z, owner_ref, pos_ref, bg_ref, grade_ref, p_ref, g_ref, slab, gbuf, sems, gsem):
    me_state, me_mem = lax.axis_index("state"), lax.axis_index("mem")
    me = me_state * z.n_mem + me_mem
    levels = pltpu.make_async_copy(grade_ref, gbuf, gsem)
    levels.start()

    def slab_copy(b):
        at = pl.multiple_of(lax.rem(owner_ref[b], z.n_mem) * z.unit, LANES)
        return pltpu.make_async_copy(bg_ref.at[:, pl.ds(at, z.unit)], slab.at[b], sems.at[b])

    here = [lax.div(owner_ref[b], z.n_mem) == me_state for b in range(z.batches)]
    for b in range(z.batches):
        pl.when(here[b])(lambda b=b: slab_copy(b).start())
    p_ref[...] = jnp.zeros_like(p_ref)
    levels.wait()
    for n, (b, c) in enumerate(z.pairs):
        mine = jnp.where(owner_ref[c] == me, 1.0, 0.0)
        g = gbuf[b].astype(jnp.float32) * mine
        g_ref[n * z.blocks:(n + 1) * z.blocks, :] = g[:, :LANES]
        half, r0 = n // (len(z.pairs) // 2), (n % (len(z.pairs) // 2)) * z.blocks + z.grade_rows
        g_ref[r0:r0 + z.blocks, half * z.tail:(half + 1) * z.tail] = g[:, LANES:]
    lane = lax.broadcasted_iota(jnp.int32, (z.rows, LANES), 1)

    def take(b):
        slab_copy(b).wait()
        first = b * z.obs
        while first < (b + 1) * z.obs:
            last = min((first // LANES + 1) * LANES, (b + 1) * z.obs)

            def body(q, acc):
                p = pos_ref[b, q - b * z.obs]
                at = pl.multiple_of(lax.div(p, LANES) * LANES, LANES)
                tile = slab[b, :, pl.ds(at, LANES)]
                to = lax.rem(q, LANES)
                tile = pltpu.roll(tile, lax.rem(to - p + at + LANES, LANES), 1)
                return jnp.where(lane == to, tile, acc)

            t = first // LANES
            acc = p_ref[t * z.rows:(t + 1) * z.rows, :]
            p_ref[t * z.rows:(t + 1) * z.rows, :] = lax.fori_loop(first, last, body, acc, unroll=16)
            first = last

    for b in range(z.batches):
        pl.when(here[b])(functools.partial(take, b))


def gather(z, owner, position, background, grade):
    return pl.pallas_call(
        functools.partial(gather_kernel, z),
        out_shape=(
            jax.ShapeDtypeStruct((z.tiles * z.rows, LANES), jnp.float32),
            jax.ShapeDtypeStruct((z.grade_rows * z.obs // LANES, LANES), jnp.float32),
        ),
        in_specs=[
            pl.BlockSpec(memory_space=pltpu.SMEM),
            pl.BlockSpec(memory_space=pltpu.SMEM),
            pl.BlockSpec(memory_space=pl.ANY),
            pl.BlockSpec(memory_space=pl.ANY),
        ],
        out_specs=(pl.BlockSpec(memory_space=pltpu.VMEM), pl.BlockSpec(memory_space=pltpu.VMEM)),
        scratch_shapes=[
            pltpu.VMEM((z.batches, z.rows, z.unit), jnp.float32),
            pltpu.VMEM(grade.shape, jnp.int32),
            pltpu.SemaphoreType.DMA((z.batches,)),
            pltpu.SemaphoreType.DMA,
        ],
        compiler_params=pltpu.CompilerParams(vmem_limit_bytes=16 * MIB),
        name="gather",
    )(owner, position, background, grade)


def pack_kernel(z, bg_ref, *refs):
    outs, rest, sem_w, sem_r = refs[:z.n_mem], refs[-3], refs[-2], refs[-1]
    me = lax.axis_index("mem")

    def copies(r):
        cols = pl.ds(pl.multiple_of(lax.bitwise_xor(me, r) * z.unit, LANES), z.unit)
        return (
            pltpu.make_async_copy(bg_ref.at[:z.whole, cols], outs[r].at[:, :z.unit], sem_w.at[r]),
            pltpu.make_async_copy(bg_ref.at[z.whole:, cols], rest.at[r], sem_r.at[r]),
        )

    order = list(range(1, z.n_mem)) + [0]
    for r in order:
        for copy in copies(r):
            copy.start()
    part = z.unit // z.fold
    for r in order:
        whole, tail = copies(r)
        tail.wait()
        for q in range(z.fold):
            outs[r][q * z.rest:(q + 1) * z.rest, z.unit:] = rest[r, :, q * part:(q + 1) * part]
        whole.wait()


def pack(z, background):
    shape = pltpu.VMEM((z.whole, z.packed), jnp.float32)
    return pl.pallas_call(
        functools.partial(pack_kernel, z),
        out_shape=[shape] * z.n_mem,
        in_specs=[pl.BlockSpec(memory_space=pl.ANY)],
        out_specs=[pl.BlockSpec(memory_space=pltpu.VMEM)] * z.n_mem,
        scratch_shapes=[
            pltpu.VMEM((z.n_mem, z.rest, z.unit), jnp.float32),
            pltpu.SemaphoreType.DMA((z.n_mem,)),
            pltpu.SemaphoreType.DMA((z.n_mem,)),
        ],
        compiler_params=pltpu.CompilerParams(vmem_limit_bytes=8 * MIB),
        name="pack",
    )(background)


def pair_lanes(x):
    return jnp.concatenate(split(x), axis=1)


def halves(x):
    return x[:, :LANES] + x[:, LANES:]


def serial_kernel(z, p_ref, g_ref, level_ref, y_ref, noise_ref, pos_ref, out_ref, pbuf, fbuf, tbuf, mbuf):
    n, scale = z.members, 1.0 / (z.members - 1)
    me = lax.axis_index("mem")
    for t in range(z.tiles):
        for m in range(z.n_mem):
            pbuf[m * z.rows:(m + 1) * z.rows, t * LANES:(t + 1) * LANES] = p_ref[m, t * z.rows:(t + 1) * z.rows, :]
    priors = [pbuf[:, b * z.obs:(b + 1) * z.obs] for b in range(z.batches)]
    row = lax.broadcasted_iota(jnp.int32, (n, LANES), 0)
    col = lax.broadcasted_iota(jnp.int32, (n, LANES), 1)
    eye = jnp.where(row == col, 1.0, 0.0)[:, :n]
    edge = z.whole * z.n_mem
    late = col >= edge
    source = jnp.where(late, lax.div(col - edge, z.rest), lax.div(col, z.whole))
    within = jnp.where(late, z.whole + lax.rem(col - edge, z.rest), lax.rem(col, z.whole))
    order = jnp.where((row == lax.bitwise_xor(source, me) * z.rows + within) & (col < n), 1.0, 0.0)
    block = lax.div(pos_ref[...], z.width)
    sub = lax.broadcasted_iota(jnp.int32, (z.blocks, z.obs), 0)
    pick = [jnp.where(sub == block[c:c + 1, :], 1.0, 0.0).astype(jnp.bfloat16) for c in range(z.batches)]

    def observed_levels(b, c):
        k = z.pairs.index((b, c))
        half, r0 = k // (len(z.pairs) // 2), (k % (len(z.pairs) // 2)) * z.blocks + z.grade_rows
        g = jnp.concatenate(
            [g_ref[k * z.blocks:(k + 1) * z.blocks, :], g_ref[r0:r0 + z.blocks, half * z.tail:(half + 1) * z.tail]], axis=1)
        return dot16(g.astype(jnp.bfloat16), pick[c], TN)

    def newton(state):
        err, acc, e = state
        both = dot32(jnp.concatenate([err, acc], axis=0), err)
        mu = 2.0 / (2.0 - e * e)
        return mu * both[:n] + (1.0 - mu) * eye, mu * (acc + both[n:]), e * e / (2.0 - e * e)

    def make_moves(b, i, gain, right):
        left = []
        for u in range(GROUP):
            high, low = split(gain * level_ref[b, pl.ds(i * GROUP + u, 1), :].astype(jnp.float32))
            left.append(jnp.concatenate([high, gap_lanes, low], axis=1))
        both = dot16(jnp.concatenate(left, axis=0), right, NT)
        for u in range(GROUP):
            move = halves(both[n * u:n * (u + 1)])
            if b == 0:
                keep(b, i * GROUP + u, order + move)
            else:
                mbuf[lax.rem(i, 2), u] = pair_lanes(move)

    def keep(b, k, new):
        high, low = split(new)
        if b + 1 < z.batches:
            fbuf[k] = new
            both = jnp.concatenate([high, low], axis=1)
            tbuf[k, :n] = both
            tbuf[k, LANES:] = both
        else:
            out_ref[k] = jnp.concatenate([high[:, :n], high[:, :n], low[:, :n]], axis=1)

    def use_moves(b, i):
        for u in range(GROUP):
            k = i * GROUP + u
            keep(b, k, fbuf[k] + halves(dot16(mbuf[lax.rem(i, 2), u][:, :LANES + n], tbuf[k])))

    groups = z.blocks // GROUP

    def blocks(b, gain, right, also, state):
        if b == 0:

            def body(i, state):
                make_moves(b, i, gain, right)
                return also(state)

            return lax.fori_loop(0, groups, body, state)
        make_moves(b, 0, gain, right)

        def body(i, state):
            use_moves(b, i)
            make_moves(b, i + 1, gain, right)
            return also(state)

        state = lax.fori_loop(0, groups - 1, body, state)
        use_moves(b, groups - 1)
        return state

    gap_lanes = jnp.zeros((n, 2 * LANES - z.obs), jnp.bfloat16)
    tbuf[:, n:LANES, :] = jnp.zeros((z.blocks, LANES - n, 2 * LANES), jnp.bfloat16)
    before = None
    for b in range(z.batches):
        prior = priors[b]
        mean = jnp.sum(prior, axis=0, keepdims=True) * (1.0 / n)
        spread = prior - mean
        innovation = y_ref[b:b + 1, :] - mean
        inv_noise = 1.0 / noise_ref[b:b + 1, :]
        weighted = spread * inv_noise
        gram = dot32(weighted, spread, NT) * scale
        shift = dot32(innovation, weighted, NT) * scale
        top = 1.0 + jnp.max(jnp.sum(jnp.abs(gram), axis=0, keepdims=True), axis=1, keepdims=True)
        first = 2.0 / (1.0 + top)
        state = (eye - first * (eye + gram), first * (0.5 * eye + shift), (top - 1.0) / (top + 1.0))
        if before is None:
            for _ in range(4):
                state = newton(state)
        else:
            state = blocks(*before, newton, state)
        err, acc, _ = lax.while_loop(lambda s: jnp.max(s[2]) > 1e-3, newton, state)
        acc = acc + dot32(acc, err)
        gain = innovation * inv_noise - dot32(acc, weighted)
        quarter = spread * (0.25 * scale)
        gain2, quarter2 = split(gain), split(quarter)
        for c in range(b + 1, z.batches):
            change = split(observed_levels(b, c) * dot3(quarter2, split(priors[c]), TN))
            priors[c] = priors[c] + dot3(gain2, change)
        gap = jnp.zeros((LANES - n, z.obs), jnp.bfloat16)
        high, low = split(dot32(order[:, :n], quarter, TN) if b == 0 else quarter)
        right = jnp.concatenate([high, gap, low, gap], axis=0)
        gap = jnp.zeros((2 * LANES, 2 * LANES - z.obs), jnp.bfloat16)
        before = (b, gain, jnp.concatenate([right, gap, right], axis=1))

    blocks(*before, lambda state: state, 0)


def serial(z, prior, grades, levels, readings, noise, position):
    vmem = pl.BlockSpec(memory_space=pltpu.VMEM)
    return pl.pallas_call(
        functools.partial(serial_kernel, z),
        out_shape=jax.ShapeDtypeStruct((z.blocks, z.members, 3 * z.members), jnp.bfloat16),
        in_specs=[vmem] * 6,
        out_specs=vmem,
        scratch_shapes=[
            pltpu.VMEM((z.members, z.tiles * LANES), jnp.float32),
            pltpu.VMEM((z.blocks, z.members, LANES), jnp.float32),
            pltpu.VMEM((z.blocks, LANES + z.members, 2 * LANES), jnp.bfloat16),
            pltpu.VMEM((2, GROUP, z.members, 2 * LANES), jnp.bfloat16),
        ],
        compiler_params=pltpu.CompilerParams(vmem_limit_bytes=20 * MIB),
        name="serial",
    )(prior, grades, levels, readings, noise, position)


def apply_kernel(z, move_ref, *refs):
    ins, out_ref, buf, sems = refs[:z.n_mem], refs[z.n_mem], refs[-2], refs[-1]
    part = z.unit // z.fold
    per = part // z.width
    for q in range(z.fold):

        def one_block(i, carry, q=q):
            at = pl.multiple_of(i * z.width, LANES)
            wide = pl.ds(q * part + at, z.width)
            rest = pl.ds(z.unit + at, z.width)
            x = jnp.concatenate(
                [r[:, wide] for r in ins] + [r[q * z.rest:(q + 1) * z.rest, rest] for r in ins], axis=0)
            k = q * per + i
            high, low = split(x)
            buf[:, wide] = dot16(move_ref[k], jnp.concatenate([high, low, high], axis=0))
            return carry

        lax.fori_loop(0, per, one_block, 0, unroll=2)
        cols = pl.ds(q * part, part)
        pltpu.make_async_copy(buf.at[:, cols], out_ref.at[:, cols], sems.at[q]).start()
    for q in range(z.fold):
        cols = pl.ds(q * part, part)
        pltpu.make_async_copy(buf.at[:, cols], out_ref.at[:, cols], sems.at[q]).wait()


def apply(z, moves, parts):
    vmem = pl.BlockSpec(memory_space=pltpu.VMEM)
    return pl.pallas_call(
        functools.partial(apply_kernel, z),
        out_shape=jax.ShapeDtypeStruct((z.members, z.unit), jnp.float32),
        in_specs=[vmem] * (1 + z.n_mem),
        out_specs=pl.BlockSpec(memory_space=pl.ANY),
        scratch_shapes=[
            pltpu.VMEM((z.members, z.unit), jnp.float32),
            pltpu.SemaphoreType.DMA((z.fold,)),
        ],
        compiler_params=pltpu.CompilerParams(vmem_limit_bytes=14 * MIB),
        name="apply",
    )(moves, *(pltpu.with_memory_space_constraint(x, pltpu.VMEM) for x in parts))


def swap(x, axis, bit, size):
    return lax.ppermute(x, axis, [(i, i ^ bit) for i in range(size)])


def share(z, prior, grades):
    me = lax.axis_index("mem")
    half = grades.shape[0] // 2
    odd = me % 2 == 1
    low, high = grades[:half], grades[half:]
    mine = jnp.where(odd, high, low) + swap(jnp.where(odd, low, high), "mem", 1, z.n_mem)
    both = jnp.concatenate([prior, mine], axis=0)
    bit = 1
    while bit < z.n_state:
        both = both + swap(both, "state", bit, z.n_state)
        bit *= 2
    prior, mine = both[:prior.shape[0]], both[prior.shape[0]:]
    there = swap(both, "mem", 2, z.n_mem)
    other, mine = there[:prior.shape[0]], mine + there[prior.shape[0]:]
    upper = me >= 2
    pair = jnp.stack([jnp.where(upper, other, prior), jnp.where(upper, prior, other)])
    rows = pair.shape[0] * pair.shape[1]
    both = jnp.concatenate([pair.reshape(rows, LANES), mine], axis=0)
    there = swap(both, "mem", 1, z.n_mem)
    pair_t = there[:rows].reshape(pair.shape)
    mine_t = there[rows:]
    even, uneven = jnp.where(odd, pair_t, pair), jnp.where(odd, pair, pair_t)
    prior = jnp.stack([even[0], uneven[0], even[1], uneven[1]])
    grades = jnp.concatenate([jnp.where(odd, mine_t, mine), jnp.where(odd, mine, mine_t)], axis=0)
    return prior, grades


def solution(mesh):
    def local(background, readings, noise, owner, position, grade):
        z = Sizes(mesh, background, position, grade)
        levels = jnp.transpose(grade, (0, 2, 1))
        parts = list(pack(z, background))
        for r in range(z.n_mem - 1, 0, -1):
            parts[r] = swap(parts[r], "mem", r, z.n_mem)
        prior, grades = gather(z, owner, position, background, levels)
        prior, grades = share(z, prior, grades)
        moves = serial(z, prior, grades, levels, readings, noise, position)
        return apply(z, moves, parts)

    return jax.shard_map(
        local,
        mesh=mesh,
        in_specs=(P("mem", "state"), P(), P(), P(), P(), P(None, None, ("state", "mem"))),
        out_specs=P(None, ("state", "mem")),
        check_vma=False,
    )
```
